32 devices in a mesh: mem: 8 (over z, x), fsdp: 4 (over y, core).
Axes of the slice: x: 2, y: 2, z: 4, core: 2. Of those that a mesh axis runs over, the one named last changes fastest.
Arguments:
- layer_input: bfloat16 [4096, 4096], P(('mem', 'fsdp')), may hold values from -6 to 6
- w_query: bfloat16 [4096, 2048], P('mem', 'fsdp'), may hold values from -0.09375 to 0.09375
- local_kv: bfloat16 [2, 4096, 2048], P(None, 'mem', 'fsdp'), may hold values from -200 to 200, as said below
- memory_kv: bfloat16 [128, 2, 128, 2048], P('mem', None, None, 'fsdp'), may hold values from -200 to 200
- memory_ids: int32 [32, 4], P('mem'), may hold values from 0 to 127, as said below
- grad_out: bfloat16 [4096, 2048], P('mem', 'fsdp'), may hold values from -6 to 6
Outputs:
- attended: bfloat16 [4096, 2048], P('mem', 'fsdp')
- grad_input: bfloat16 [4096, 4096], P(('mem', 'fsdp'))
The draws below stay inside these ranges and needn't reach their ends.
Inputs may be any that keep to these rules, and one draw needn't show every extreme that they name: `memory_ids`: within the tiles of one local context (4 tiles), all named blocks of one owner (same id // 16) are one and the same block, and every owner is named by some tile of every local context; each tile names 4 blocks of different owners. `local_kv`: keys and values of the document's tokens.
All inputs are finite; a program needn't handle non-finite values.
Results may differ from the reference program's by a relative error of at most 0.025.
The reference program's roundings to bfloat16 on the way count: a program that leaves them out, or rounds other values in their place, can miss the bound.
Values may be sent and summed in bfloat16 or wider, within the bound.
A program may use at most 128 MiB of HBM per device.

```python
import math
import jax
import jax.numpy as jnp
from jax import lax

D = 4096
HD = 128
BLK = 128
TOPK = 4
MB_DEV = 16
HW = 2048
CTX = 512
LEN = 4096
TILES = 32
MEMBLK = 128
N_FSDP = 4


def key_rows(key, rows_count, width):
    first_key = jax.random.fold_in(key, 0)
    return jnp.clip(jax.random.normal(first_key, (rows_count, width), jnp.float32), -4.0, 4.0)


def value_rows(key, rows_count, width):
    return jnp.clip(jax.random.normal(key, (rows_count, width), jnp.float32), -4.0, 4.0)


def draw_local_kv(key, part):
    keys_part = key_rows(jax.random.fold_in(key, 11), LEN, HW)
    values_part = value_rows(jax.random.fold_in(key, 12), LEN, HW)
    return jnp.stack([keys_part, values_part]).astype(jnp.bfloat16)


def draw_memory_kv(key, part):
    keys_part = key_rows(jax.random.fold_in(key, 21), MEMBLK * BLK, HW).reshape(MEMBLK, BLK, HW)
    values_part = value_rows(jax.random.fold_in(key, 22), MEMBLK * BLK, HW).reshape(MEMBLK, BLK, HW)
    return jnp.stack([keys_part, values_part], axis=1).astype(jnp.bfloat16)


def draw_memory_ids(key, part):
    owners_count = MEMBLK // MB_DEV
    groups = LEN // CTX
    tiles_per_group = CTX // BLK
    slots_count = tiles_per_group * TOPK
    first_key, second_key, third_key = jax.random.split(jax.random.fold_in(key, 31), 3)
    local_pick = jax.random.randint(first_key, (groups, owners_count), 0, MB_DEV)
    group_keys = jax.random.split(second_key, groups)
    orders = jax.vmap(lambda one_key: jax.random.permutation(one_key, owners_count))(group_keys).astype(jnp.int32)
    rotation = jax.random.randint(third_key, (groups, 1), 0, owners_count)
    slot_index = jnp.arange(slots_count, dtype=jnp.int32)
    positions = (slot_index[None, :] + rotation) % owners_count
    owners = jnp.take_along_axis(orders, positions, axis=1)
    local_part = jnp.take_along_axis(local_pick, owners, axis=1)
    block_ids = owners * MB_DEV + local_part
    return block_ids.reshape(TILES, TOPK).astype(jnp.int32)


def block_scale(own_key, shape, cuts, smallest, top_value):
    level, own = 1.0, jax.random.fold_in(own_key, 6)
    for position, parts in cuts:
        steps = jnp.exp(jax.random.uniform(jax.random.fold_in(own, position), (parts,), jnp.float32, smallest / len(cuts), top_value / len(cuts)))
        level = level * jnp.repeat(steps, shape[position] // parts).reshape([-1 if axis == position else 1 for axis in range(len(shape))])
    return level


def centred(own_key, extent, spread, most, cuts=(), kind=jnp.bfloat16):
    factor_of = block_scale(own_key, extent, cuts, -0.22, 0.18) if cuts else 1.0
    drawn = jax.random.normal(own_key, extent, jnp.float32) * spread * factor_of
    return jnp.minimum(jnp.maximum(drawn, -most), most).astype(kind)


def setup_inputs(seed: int = 0) -> dict:
    key_of = jax.random.split(jax.random.key(seed), 7)
    layer_input = centred(key_of[0], (LEN, D), 1.0, 6.0, ((0, 32),))
    w_query = centred(key_of[1], (D, HW), D ** -0.5, 0.09375, ((0, 8), (1, 4)))
    local_kv = draw_local_kv(jax.random.fold_in(key_of[6], 71), 0)
    memory_kv = draw_memory_kv(jax.random.fold_in(key_of[6], 71), 0)
    memory_ids = draw_memory_ids(jax.random.fold_in(key_of[6], 71), 0)
    grad_out = centred(key_of[5], (LEN, HW), 1.0, 6.0, ((0, 8), (1, 4)))
    return dict(layer_input=layer_input, w_query=w_query, local_kv=local_kv, memory_kv=memory_kv, memory_ids=memory_ids, grad_out=grad_out)


NEG_FILL = -1e+30

def attend_context(queries, context_kv, tile_kv, grad_rows):
    ctx_len, width = queries.shape
    heads_count = width // HD
    tiles_count = tile_kv.shape[0]
    mem_keys_count = TOPK * BLK
    score_scale = 1.0 / math.sqrt(HD)
    query_heads = queries.astype(jnp.float32).reshape(ctx_len, heads_count, HD)
    query_tiles = query_heads.reshape(tiles_count, BLK, heads_count, HD)
    local_keys = context_kv[0].astype(jnp.float32).reshape(ctx_len, heads_count, HD)
    local_values = context_kv[1].astype(jnp.float32).reshape(ctx_len, heads_count, HD)
    mem_keys = tile_kv[:, :, 0].astype(jnp.float32).reshape(tiles_count, mem_keys_count, heads_count, HD)
    mem_values = tile_kv[:, :, 1].astype(jnp.float32).reshape(tiles_count, mem_keys_count, heads_count, HD)
    grad_heads = grad_rows.astype(jnp.float32).reshape(ctx_len, heads_count, HD)
    grad_tiles = grad_heads.reshape(tiles_count, BLK, heads_count, HD)
    mem_scores = jnp.einsum('tqhd,tkhd->htqk', query_tiles, mem_keys) * score_scale
    mem_scores = mem_scores.reshape(heads_count, ctx_len, mem_keys_count)
    loc_scores = jnp.einsum('qhd,khd->hqk', query_heads, local_keys) * score_scale
    positions = jnp.arange(ctx_len, dtype=jnp.int32)
    causal = positions[:, None] >= positions[None, :]
    loc_scores = jnp.where(causal[None], loc_scores, NEG_FILL)
    row_max = jnp.maximum(lax.optimization_barrier(jnp.max(mem_scores, axis=2)), lax.optimization_barrier(jnp.max(loc_scores, axis=2)))
    mem_exp = jnp.exp(mem_scores - row_max[:, :, None])
    loc_exp = jnp.exp(loc_scores - row_max[:, :, None])
    total = lax.optimization_barrier(jnp.sum(mem_exp, axis=2)) + lax.optimization_barrier(jnp.sum(loc_exp, axis=2))
    mem_prob = mem_exp / total[:, :, None]
    loc_prob = loc_exp / total[:, :, None]
    mem_weights = lax.optimization_barrier(mem_prob.astype(jnp.bfloat16)).astype(jnp.float32)
    loc_weights = lax.optimization_barrier(loc_prob.astype(jnp.bfloat16)).astype(jnp.float32)
    mem_part = jnp.einsum('htqk,tkhd->tqhd', mem_weights.reshape(heads_count, tiles_count, BLK, mem_keys_count), mem_values)
    loc_part = jnp.einsum('hqk,khd->qhd', loc_weights, local_values)
    attended = (mem_part.reshape(ctx_len, heads_count, HD) + loc_part).reshape(ctx_len, width).astype(jnp.bfloat16)
    mem_dprob = jnp.einsum('tqhd,tkhd->htqk', grad_tiles, mem_values).reshape(heads_count, ctx_len, mem_keys_count)
    loc_dprob = jnp.einsum('qhd,khd->hqk', grad_heads, local_values)
    delta = lax.optimization_barrier(jnp.sum(mem_prob * mem_dprob, axis=2)) + lax.optimization_barrier(jnp.sum(loc_prob * loc_dprob, axis=2))
    mem_dscore = (mem_prob * (mem_dprob - delta[:, :, None])).astype(jnp.bfloat16)
    loc_dscore = (loc_prob * (loc_dprob - delta[:, :, None])).astype(jnp.bfloat16)
    mem_dscore = lax.optimization_barrier(mem_dscore).astype(jnp.float32)
    loc_dscore = lax.optimization_barrier(loc_dscore).astype(jnp.float32)
    mem_grad = jnp.einsum('htqk,tkhd->tqhd', mem_dscore.reshape(heads_count, tiles_count, BLK, mem_keys_count), mem_keys)
    loc_grad = jnp.einsum('hqk,khd->qhd', loc_dscore, local_keys)
    grad_queries = ((mem_grad.reshape(ctx_len, heads_count, HD) + loc_grad) * score_scale).reshape(ctx_len, width)
    return (attended, grad_queries.astype(jnp.bfloat16))

def reference(layer_input, w_query, local_kv, memory_kv, memory_ids, grad_out):
    queries = jnp.dot(layer_input, w_query, preferred_element_type=jnp.float32).astype(jnp.bfloat16)
    tiles_per_context = CTX // BLK

    def one_context(context_index):
        row_first = (context_index * CTX).astype(jnp.int32)
        tile_first = (context_index * tiles_per_context).astype(jnp.int32)
        query_rows = lax.dynamic_slice_in_dim(queries, row_first, CTX, 0)
        context_kv = lax.dynamic_slice_in_dim(local_kv, row_first, CTX, 1)
        grad_rows = lax.dynamic_slice_in_dim(grad_out, row_first, CTX, 0)
        block_ids = lax.dynamic_slice_in_dim(memory_ids, tile_first, tiles_per_context, 0)
        tile_kv = jnp.take(memory_kv, block_ids, axis=0)
        return attend_context(query_rows, context_kv, tile_kv, grad_rows)
    attended, grad_queries = lax.map(one_context, jnp.arange(LEN // CTX, dtype=jnp.int32))
    attended = attended.reshape(LEN, HW)
    grad_queries = grad_queries.reshape(LEN, HW)
    group_cols = HW // N_FSDP
    grad_total = jnp.zeros((LEN, D), jnp.float32)
    for group in range(N_FSDP):
        grad_cols = grad_queries[:, group * group_cols:(group + 1) * group_cols]
        weight_cols = w_query[:, group * group_cols:(group + 1) * group_cols]
        partial_sum = lax.dot_general(grad_cols, weight_cols, (((1,), (1,)), ((), ())), preferred_element_type=jnp.float32)
        grad_total = grad_total + lax.optimization_barrier(partial_sum.astype(jnp.bfloat16)).astype(jnp.float32)
    return (attended, grad_total.astype(jnp.bfloat16))
```

```python
import functools
import math

import jax
import jax.numpy as jnp
from jax import lax
from jax.experimental import pallas as pl
from jax.experimental.pallas import tpu as pltpu
from jax.sharding import PartitionSpec as P

HD = 128
BLK = 128
NEG_FILL = -1e30
MESH = pl.DeviceIdType.MESH
NT = (((1,), (1,)), ((), ()))


def dot_nn(a, b):
    return jnp.dot(a, b, preferred_element_type=jnp.float32)


def dot_nt(a, b):
    return lax.dot_general(a, b, NT, preferred_element_type=jnp.float32)


def kernel(
    n, nx, nf, topk, mb_dev,
    ids_s, ids_v, x_hbm, w_hbm, lkv_hbm, mkv_hbm, go_hbm,
    att_ref, gin_ref,
    wf, xf, kv, lkv, go, outbox, inbox, ids_in, ids_sm, q32, qb, gq,
    p_send, p_own, s_recv, y_send, y_recv,
    l_sem, i_send, i_recv, i_loc, w_up, w_down, w_x, w_recv, wx_recv,
    x_ysend, x_ssend, x_recv, m_send, m_recv, r_ssend, r_srecv, r_ysend, r_yrecv,
):
    me = lax.axis_index("mem")
    mf = lax.axis_index("fsdp")
    nz = n // nx
    z, xx = me // nx, lax.rem(me, nx)
    ny = nf // 2
    yy, cc = mf // 2, lax.rem(mf, 2)
    sib = mf + 1 - 2 * cc
    dk = wf.shape[1]
    width = wf.shape[2]
    heads = width // HD
    tiles = ids_s.shape[0]
    rows_dev = xf.shape[0] // nf
    ctx = xf.shape[0]

    def local_copy(src, dst, k):
        return pltpu.make_async_copy(src, dst, l_sem.at[k])

    own_x = pl.ds(pl.multiple_of(mf * rows_dev, rows_dev), rows_dev)
    c_w = local_copy(w_hbm, wf.at[me], 0)
    c_x = local_copy(x_hbm, xf.at[own_x, :], 1)
    c_kv = local_copy(mkv_hbm, kv, 2)
    c_lkv = local_copy(lkv_hbm, lkv, 3)
    c_go = local_copy(go_hbm, go, 4)
    c_w.start()
    c_x.start()
    c_kv.start()
    c_lkv.start()
    c_go.start()

    barrier = pltpu.get_barrier_semaphore()

    @pl.loop(1, n)
    def _(d):
        pl.semaphore_signal(
            barrier, inc=1, device_id=(lax.rem(me + d, n), mf), device_id_type=MESH
        )

    pl.semaphore_signal(barrier, inc=1, device_id=(me, sib), device_id_type=MESH)
    for d in range(1, ny):
        pl.semaphore_signal(
            barrier, inc=1, device_id=(me, lax.rem(mf + 2 * d, nf)), device_id_type=MESH
        )
    pl.semaphore_wait(barrier, n - 1 + 1 + ny - 1)

    def remote(src, dst, s, r, dm, df):
        return pltpu.make_async_remote_copy(
            src_ref=src, dst_ref=dst, send_sem=s, recv_sem=r,
            device_id=(dm, df), device_id_type=MESH,
        )

    def id_copy(peer, slot):
        return remote(ids_v, inbox.at[slot], i_send.at[peer], i_recv.at[slot], peer, mf)

    @pl.loop(1, n)
    def _(d):
        id_copy(lax.rem(me + d, n), me).start()

    def w_copy(slot, sem, dst_m, rsem):
        return remote(wf.at[slot], wf.at[slot], sem, rsem, dst_m, mf)

    def w_up_copy(zz):
        return w_copy(zz * nx + xx, w_up.at[zz], me + nx, w_recv.at[zz])

    def w_down_copy(zz):
        return w_copy(zz * nx + xx, w_down.at[zz], me - nx, w_recv.at[zz])

    x_next = z * nx + lax.rem(xx + 1, nx)

    def w_x_copy(r, zz):
        slot = zz * nx + lax.rem(xx - r + nx, nx)
        return w_copy(slot, w_x.at[r, zz], x_next, wx_recv.at[r, zz])

    def w_x_arrival(r, zz):
        slot = zz * nx + lax.rem(xx - 1 - r + 2 * nx, nx)
        return w_copy(slot, w_x.at[r, zz], x_next, wx_recv.at[r, zz])

    c_w.wait()

    @pl.when(z + 1 < nz)
    def _():
        w_up_copy(z).start()

    @pl.when(z > 0)
    def _():
        w_down_copy(z).start()

    w_x_copy(0, z).start()
    c_x.wait()

    def x_rows(f):
        return xf.at[pl.ds(pl.multiple_of(f * rows_dev, rows_dev), rows_dev), :]

    def x_ycopy(d):
        return remote(
            x_rows(mf), x_rows(mf), x_ysend.at[d], x_recv.at[mf], me, lax.rem(mf + 2 * d, nf)
        )

    def x_scopy(f):
        return remote(x_rows(f), x_rows(f), x_ssend.at[f], x_recv.at[f], me, sib)

    for d in range(1, ny):
        x_ycopy(d).start()
    x_scopy(mf).start()

    for k in range(1, nz):
        @pl.when(z - k >= 0)
        def _():
            w_up_copy(z - k).wait_recv()

            @pl.when(z + 1 < nz)
            def _():
                w_up_copy(z - k).start()

            w_x_copy(0, z - k).start()

        @pl.when(z + k < nz)
        def _():
            w_down_copy(z + k).wait_recv()

            @pl.when(z > 0)
            def _():
                w_down_copy(z + k).start()

            w_x_copy(0, z + k).start()

        if k == 1:
            @pl.loop(1, n)
            def _(d):
                src = lax.rem(me + d, n)
                id_copy(src, src).wait_recv()

            c_ids = pltpu.make_async_copy(inbox, ids_sm, i_loc.at[0])
            c_ids.start()
            c_kv.wait()
            c_ids.wait()

            @pl.loop(1, n)
            def _(d):
                peer = lax.rem(me + d, n)
                want = jnp.int32(0)
                for j in range(tiles * topk):
                    one = ids_sm[peer, 0, j]
                    want = jnp.where(one // mb_dev == me, lax.rem(one, mb_dev), want)
                outbox[peer] = kv[want]

            @pl.loop(1, n)
            def _(d):
                peer = lax.rem(me + d, n)
                remote(
                    outbox.at[peer], ids_in.at[me], m_send.at[peer], m_recv.at[me], peer, mf
                ).start()

            mine = jnp.int32(0)
            for j in range(tiles * topk):
                one = ids_s[j // topk, j % topk]
                mine = jnp.where(one // mb_dev == me, lax.rem(one, mb_dev), mine)
            ids_in[me] = kv[mine]

    for d in range(1, ny):
        f = lax.rem(mf + 2 * d, nf)
        x_scopy(f).wait_recv()
        x_scopy(f).start()
    for r in range(nx - 1):
        for zz in range(nz):
            w_x_arrival(r, zz).wait_recv()
            if r + 1 < nx - 1:
                w_x_copy(r + 1, zz).start()
    for d in range(ny):
        x_scopy(lax.rem(sib + 2 * d, nf)).wait_recv()

    q32[...] = jnp.zeros_like(q32)

    @pl.loop(0, n)
    def _(m):
        q32[...] += dot_nn(xf[:, pl.ds(pl.multiple_of(m * dk, dk), dk)], wf[m])

    qb[...] = q32[...].astype(jnp.bfloat16)
    c_lkv.wait()
    c_go.wait()

    @pl.loop(1, n)
    def _(d):
        src = lax.rem(me + d, n)
        remote(
            outbox.at[src], ids_in.at[src], m_send.at[src], m_recv.at[src], src, mf
        ).wait_recv()

    scale = 1.0 / math.sqrt(HD)

    @pl.loop(0, tiles)
    def _(t):
        rows = pl.ds(pl.multiple_of(t * BLK, BLK), BLK)
        owners = [ids_s[t, j] // mb_dev for j in range(topk)]
        causal = lax.broadcasted_iota(jnp.int32, (BLK, ctx), 0) + t * BLK >= (
            lax.broadcasted_iota(jnp.int32, (BLK, ctx), 1)
        )

        @pl.loop(0, heads)
        def _(h):
            cols = pl.ds(pl.multiple_of(h * HD, HD), HD)
            q = qb[rows, cols]
            g = go[rows, cols]
            keys = [ids_in[o, 0, :, cols] for o in owners]
            vals = [ids_in[o, 1, :, cols] for o in owners]
            mk = jnp.concatenate(keys, axis=0)
            mv = jnp.concatenate(vals, axis=0)
            lk = lkv[0, :, cols]
            lv = lkv[1, :, cols]
            s_m = dot_nt(q, mk) * scale
            s_l = jnp.where(causal, dot_nt(q, lk) * scale, NEG_FILL)
            top = jnp.maximum(
                jnp.max(s_m, axis=1, keepdims=True), jnp.max(s_l, axis=1, keepdims=True)
            )
            e_m = jnp.exp(s_m - top)
            e_l = jnp.exp(s_l - top)
            inv = 1.0 / (
                jnp.sum(e_m, axis=1, keepdims=True) + jnp.sum(e_l, axis=1, keepdims=True)
            )
            p_m = e_m * inv
            p_l = e_l * inv
            att_ref[rows, cols] = (
                dot_nn(p_m.astype(jnp.bfloat16), mv) + dot_nn(p_l.astype(jnp.bfloat16), lv)
            ).astype(jnp.bfloat16)
            d_m = dot_nt(g, mv)
            d_l = dot_nt(g, lv)
            delta = jnp.sum(p_m * d_m, axis=1, keepdims=True) + jnp.sum(
                p_l * d_l, axis=1, keepdims=True
            )
            ds_m = (p_m * (d_m - delta)).astype(jnp.bfloat16)
            ds_l = (p_l * (d_l - delta)).astype(jnp.bfloat16)
            gq[rows, cols] = ((dot_nn(ds_m, mk) + dot_nn(ds_l, lk)) * scale).astype(jnp.bfloat16)

    def rs_s(d):
        return remote(p_send.at[d], s_recv.at[d], r_ssend.at[d], r_srecv.at[d], me, sib)

    def rs_y(d):
        return remote(
            y_send.at[d], y_recv.at[d], r_ysend.at[d], r_yrecv.at[d], me,
            lax.rem(mf + 2 * d, nf),
        )

    def share(f, dst, d):
        grad = gq[pl.ds(pl.multiple_of(f * rows_dev, rows_dev), rows_dev), :]

        @pl.loop(0, n)
        def _(m):
            dst[d, m] = dot_nt(grad, wf[m]).astype(jnp.bfloat16)

    order = list(range(1, ny)) + [0]
    for d in order:
        share(lax.rem(sib + 2 * d, nf), p_send, d)
        rs_s(d).start()
    for d in order:
        share(lax.rem(mf + 2 * d, nf), p_own, d)
        rs_s(d).wait_recv()
        if d:
            y_send[d] = (
                p_own[d].astype(jnp.float32) + s_recv[d].astype(jnp.float32)
            ).astype(jnp.bfloat16)
            rs_y(d).start()
    for d in range(1, ny):
        rs_y(d).wait_recv()
    for m in range(n):
        total = p_own[0, m].astype(jnp.float32) + s_recv[0, m].astype(jnp.float32)
        for d in range(1, ny):
            total = total + y_recv[d, m].astype(jnp.float32)
        gin_ref[:, m * dk:(m + 1) * dk] = total.astype(jnp.bfloat16)

    @pl.loop(1, n)
    def _(d):
        peer = lax.rem(me + d, n)
        id_copy(peer, me).wait_send()
        remote(
            outbox.at[peer], ids_in.at[me], m_send.at[peer], m_recv.at[me], peer, mf
        ).wait_send()

    for zz in range(nz):
        @pl.when((zz <= z) & (z + 1 < nz))
        def _():
            w_up_copy(zz).wait_send()

        @pl.when((zz >= z) & (z > 0))
        def _():
            w_down_copy(zz).wait_send()

        for r in range(nx - 1):
            w_x_copy(r, zz).wait_send()
    for d in range(ny):
        if d:
            x_ycopy(d).wait_send()
            rs_y(d).wait_send()
        x_scopy(lax.rem(mf + 2 * d, nf)).wait_send()
        rs_s(d).wait_send()


def local(n, nf, layer_input, w_query, local_kv, memory_kv, memory_ids, grad_out):
    nx = 2 ** ((n.bit_length() - 1) // 2)
    nz = n // nx
    ny = nf // 2
    rows_dev, d_model = layer_input.shape
    dk, width = w_query.shape
    ctx = rows_dev * nf
    tiles, topk = memory_ids.shape
    mb_dev = memory_kv.shape[0]
    flat = memory_ids.reshape(1, tiles * topk)
    ids_v = jnp.pad(flat, ((0, 7), (0, 128 - tiles * topk)))
    bf, f32, i32 = jnp.bfloat16, jnp.float32, jnp.int32
    any_spec = pl.BlockSpec(memory_space=pl.ANY)
    vmem_spec = pl.BlockSpec(memory_space=pltpu.VMEM)
    dma = pltpu.SemaphoreType.DMA
    part = pltpu.VMEM((ny, n, rows_dev, dk), bf)
    return pl.pallas_call(
        functools.partial(kernel, n, nx, nf, topk, mb_dev),
        out_shape=(
            jax.ShapeDtypeStruct((ctx, width), bf),
            jax.ShapeDtypeStruct((rows_dev, d_model), bf),
        ),
        in_specs=[pl.BlockSpec(memory_space=pltpu.SMEM), vmem_spec] + [any_spec] * 5,
        out_specs=(vmem_spec, vmem_spec),
        scratch_shapes=[
            pltpu.VMEM((n, dk, width), bf),
            pltpu.VMEM((ctx, d_model), bf),
            pltpu.VMEM(memory_kv.shape, bf),
            pltpu.VMEM(local_kv.shape, bf),
            pltpu.VMEM(grad_out.shape, bf),
            pltpu.VMEM((n,) + memory_kv.shape[1:], bf),
            pltpu.VMEM((n, 8, 128), i32),
            pltpu.VMEM((n,) + memory_kv.shape[1:], bf),
            pltpu.SMEM((n, 8, 128), i32),
            pltpu.VMEM((ctx, width), f32),
            pltpu.VMEM((ctx, width), bf),
            pltpu.VMEM((ctx, width), bf),
            part, part, part, part, part,
            dma((5,)), dma((n,)), dma((n,)), dma((1,)),
            dma((nz,)), dma((nz,)), dma((max(nx - 1, 1), nz)), dma((nz,)),
            dma((max(nx - 1, 1), nz)),
            dma((ny,)), dma((nf,)), dma((nf,)), dma((n,)), dma((n,)),
            dma((ny,)), dma((ny,)), dma((ny,)), dma((ny,)),
        ],
        compiler_params=pltpu.CompilerParams(
            collective_id=0, has_side_effects=True, vmem_limit_bytes=62 * 1024 * 1024
        ),
    )(memory_ids, ids_v, layer_input, w_query, local_kv, memory_kv, grad_out)


def solution(mesh):
    placed = (
        P(("mem", "fsdp"), None),
        P("mem", "fsdp"),
        P(None, "mem", "fsdp"),
        P("mem", None, None, "fsdp"),
        P("mem", None),
        P("mem", "fsdp"),
    )
    return jax.shard_map(
        functools.partial(local, mesh.shape["mem"], mesh.shape["fsdp"]),
        mesh=mesh,
        in_specs=placed,
        out_specs=(P("mem", "fsdp"), P(("mem", "fsdp"), None)),
        check_vma=False,
    )
```

```python
import functools
import math

import jax
import jax.numpy as jnp
from jax import lax
from jax.experimental import pallas as pl
from jax.experimental.pallas import tpu as pltpu
from jax.sharding import PartitionSpec as P

HD = 128
BLK = 128
NEG_FILL = -1e30
MESH = pl.DeviceIdType.MESH
NT = (((1,), (1,)), ((), ()))


def dot_nn(a, b):
    return jnp.dot(a, b, preferred_element_type=jnp.float32)


def dot_nt(a, b):
    return lax.dot_general(a, b, NT, preferred_element_type=jnp.float32)


def kernel(
    n, nx, nf, topk, mb_dev, pre, parts,
    ids_s, ids_v, x_hbm, w_hbm, lkv_hbm, mkv_hbm, go_hbm,
    att_ref, gin_ref,
    wf, xf, kv, lkv, go, outbox, inbox, ids_in, ids_sm, q32, qb, gq,
    p_send, p_own, s_recv, y_send, y_recv, s_mem, d_mem, s_loc, d_loc,
    l_sem, i_send, i_recv, i_loc, w_up, w_down, w_x, w_recv, wx_recv,
    x_ysend, x_ssend, x_recv, m_send, m_recv, r_ssend, r_srecv, r_ysend, r_yrecv,
):
    me = lax.axis_index("mem")
    mf = lax.axis_index("fsdp")
    nz = n // nx
    z, xx = me // nx, lax.rem(me, nx)
    ny = nf // 2
    yy, cc = mf // 2, lax.rem(mf, 2)
    sib = mf + 1 - 2 * cc
    dk = wf.shape[1]
    width = wf.shape[2]
    heads = width // HD
    tiles = ids_s.shape[0]
    rows_dev = xf.shape[0] // nf
    ctx = xf.shape[0]

    def local_copy(src, dst, k):
        return pltpu.make_async_copy(src, dst, l_sem.at[k])

    own_x = pl.ds(pl.multiple_of(mf * rows_dev, rows_dev), rows_dev)
    c_w = local_copy(w_hbm, wf.at[me], 0)
    c_x = local_copy(x_hbm, xf.at[own_x, :], 1)
    c_kv = local_copy(mkv_hbm, kv, 2)
    c_lkv = local_copy(lkv_hbm, lkv, 3)
    c_go = local_copy(go_hbm, go, 4)
    c_w.start()
    c_x.start()
    c_kv.start()
    c_lkv.start()
    c_go.start()

    barrier = pltpu.get_barrier_semaphore()

    @pl.loop(1, n)
    def _(d):
        pl.semaphore_signal(
            barrier, inc=1, device_id=(lax.rem(me + d, n), mf), device_id_type=MESH
        )

    pl.semaphore_signal(barrier, inc=1, device_id=(me, sib), device_id_type=MESH)
    for d in range(1, ny):
        pl.semaphore_signal(
            barrier, inc=1, device_id=(me, lax.rem(mf + 2 * d, nf)), device_id_type=MESH
        )
    pl.semaphore_wait(barrier, n - 1 + 1 + ny - 1)

    def remote(src, dst, s, r, dm, df):
        return pltpu.make_async_remote_copy(
            src_ref=src, dst_ref=dst, send_sem=s, recv_sem=r,
            device_id=(dm, df), device_id_type=MESH,
        )

    def id_copy(peer, slot):
        return remote(ids_v, inbox.at[slot], i_send.at[peer], i_recv.at[slot], peer, mf)

    @pl.loop(1, n)
    def _(d):
        id_copy(lax.rem(me + d, n), me).start()

    def w_copy(slot, sem, dst_m, rsem):
        return remote(wf.at[slot], wf.at[slot], sem, rsem, dst_m, mf)

    def w_up_copy(zz):
        return w_copy(zz * nx + xx, w_up.at[zz], me + nx, w_recv.at[zz])

    def w_down_copy(zz):
        return w_copy(zz * nx + xx, w_down.at[zz], me - nx, w_recv.at[zz])

    x_next = z * nx + lax.rem(xx + 1, nx)

    def w_x_copy(r, zz):
        slot = zz * nx + lax.rem(xx - r + nx, nx)
        return w_copy(slot, w_x.at[r, zz], x_next, wx_recv.at[r, zz])

    def w_x_arrival(r, zz):
        slot = zz * nx + lax.rem(xx - 1 - r + 2 * nx, nx)
        return w_copy(slot, w_x.at[r, zz], x_next, wx_recv.at[r, zz])

    c_w.wait()

    @pl.when(z + 1 < nz)
    def _():
        w_up_copy(z).start()

    @pl.when(z > 0)
    def _():
        w_down_copy(z).start()

    w_x_copy(0, z).start()
    c_x.wait()

    def x_rows(f):
        return xf.at[pl.ds(pl.multiple_of(f * rows_dev, rows_dev), rows_dev), :]

    def x_ycopy(d):
        return remote(
            x_rows(mf), x_rows(mf), x_ysend.at[d], x_recv.at[mf], me, lax.rem(mf + 2 * d, nf)
        )

    def x_scopy(f):
        return remote(x_rows(f), x_rows(f), x_ssend.at[f], x_recv.at[f], me, sib)

    for d in range(1, ny):
        x_ycopy(d).start()
    x_scopy(mf).start()

    @pl.loop(1, n)
    def _(d):
        src = lax.rem(me + d, n)
        id_copy(src, src).wait_recv()

    c_ids = pltpu.make_async_copy(inbox, ids_sm, i_loc.at[0])
    c_ids.start()
    c_kv.wait()
    c_ids.wait()

    @pl.loop(1, n)
    def _(d):
        peer = lax.rem(me + d, n)
        want = jnp.int32(0)
        for j in range(tiles * topk):
            one = ids_sm[peer, 0, j]
            want = jnp.where(one // mb_dev == me, lax.rem(one, mb_dev), want)
        outbox[peer] = kv[want]

    mine = jnp.int32(0)
    for j in range(tiles * topk):
        one = ids_s[j // topk, j % topk]
        mine = jnp.where(one // mb_dev == me, lax.rem(one, mb_dev), mine)
    ids_in[me] = kv[mine]

    def block_copy(peer, slot):
        return remote(
            outbox.at[peer], ids_in.at[slot], m_send.at[peer], m_recv.at[slot], peer, mf
        )

    def send_blocks(k):
        @pl.loop(1, n)
        def _(d):
            peer = lax.rem(me + d, n)
            pz = peer // nx
            up = (pz > z) & (jnp.maximum(z, 1) == k)
            down = (pz < z) & (jnp.maximum(nz - 1 - z, 1) == k)
            level = (pz == z) & (k == nz - 1)

            @pl.when(up | down | level)
            def _():
                block_copy(peer, me).start()

    for k in range(1, nz):
        @pl.when(z - k >= 0)
        def _():
            w_up_copy(z - k).wait_recv()

            @pl.when(z + 1 < nz)
            def _():
                w_up_copy(z - k).start()

            w_x_copy(0, z - k).start()

        @pl.when(z + k < nz)
        def _():
            w_down_copy(z + k).wait_recv()

            @pl.when(z > 0)
            def _():
                w_down_copy(z + k).start()

            w_x_copy(0, z + k).start()

        send_blocks(k)

    for d in range(1, ny):
        f = lax.rem(mf + 2 * d, nf)
        x_scopy(f).wait_recv()
        x_scopy(f).start()
    for r in range(nx - 1):
        for zz in range(nz):
            w_x_arrival(r, zz).wait_recv()
            if r + 1 < nx - 1:
                w_x_copy(r + 1, zz).start()
    for d in range(ny):
        x_scopy(lax.rem(sib + 2 * d, nf)).wait_recv()

    q32[...] = jnp.zeros_like(q32)

    @pl.loop(0, n)
    def _(m):
        q32[...] += dot_nn(xf[:, pl.ds(pl.multiple_of(m * dk, dk), dk)], wf[m])

    qb[...] = q32[...].astype(jnp.bfloat16)
    c_lkv.wait()
    c_go.wait()

    scale = 1.0 / math.sqrt(HD)

    def head_cols(h):
        return pl.ds(pl.multiple_of(h * HD, HD), HD)

    def block_scores(o):
        @pl.loop(0, heads)
        def _(h):
            cols = head_cols(h)
            s_mem[h, o] = dot_nt(qb[:, cols], ids_in[o, 0, :, cols]) * scale
            d_mem[h, o] = dot_nt(go[:, cols], ids_in[o, 1, :, cols])

    if pre:
        @pl.loop(0, heads)
        def _(h):
            cols = head_cols(h)
            causal = lax.broadcasted_iota(jnp.int32, (ctx, ctx), 0) >= (
                lax.broadcasted_iota(jnp.int32, (ctx, ctx), 1)
            )
            s_loc[h] = jnp.where(causal, dot_nt(qb[:, cols], lkv[0, :, cols]) * scale, NEG_FILL)
            d_loc[h] = dot_nt(go[:, cols], lkv[1, :, cols])

        block_scores(me)

    @pl.loop(1, n)
    def _(d):
        src = lax.rem(me + d, n)
        block_copy(src, src).wait_recv()
        if pre:
            block_scores(src)

    def attend(t):
        rows = pl.ds(pl.multiple_of(t * BLK, BLK), BLK)
        owners = [ids_s[t, j] // mb_dev for j in range(topk)]

        @pl.loop(0, heads)
        def _(h):
            cols = head_cols(h)
            mk = jnp.concatenate([ids_in[o, 0, :, cols] for o in owners], axis=0)
            mv = jnp.concatenate([ids_in[o, 1, :, cols] for o in owners], axis=0)
            lk = lkv[0, :, cols]
            lv = lkv[1, :, cols]
            if pre:
                s_m = jnp.concatenate([s_mem[h, o, rows, :] for o in owners], axis=1)
                d_m = jnp.concatenate([d_mem[h, o, rows, :] for o in owners], axis=1)
                s_l = s_loc[h, rows, :]
                d_l = d_loc[h, rows, :]
            else:
                q = qb[rows, cols]
                g = go[rows, cols]
                causal = lax.broadcasted_iota(jnp.int32, (BLK, ctx), 0) + t * BLK >= (
                    lax.broadcasted_iota(jnp.int32, (BLK, ctx), 1)
                )
                s_m = dot_nt(q, mk) * scale
                s_l = jnp.where(causal, dot_nt(q, lk) * scale, NEG_FILL)
                d_m = dot_nt(g, mv)
                d_l = dot_nt(g, lv)
            top = jnp.maximum(
                jnp.max(s_m, axis=1, keepdims=True), jnp.max(s_l, axis=1, keepdims=True)
            )
            e_m = jnp.exp(s_m - top)
            e_l = jnp.exp(s_l - top)
            inv = 1.0 / (
                jnp.sum(e_m, axis=1, keepdims=True) + jnp.sum(e_l, axis=1, keepdims=True)
            )
            p_m = e_m * inv
            p_l = e_l * inv
            att_ref[rows, cols] = (
                dot_nn(p_m.astype(jnp.bfloat16), mv) + dot_nn(p_l.astype(jnp.bfloat16), lv)
            ).astype(jnp.bfloat16)
            delta = jnp.sum(p_m * d_m, axis=1, keepdims=True) + jnp.sum(
                p_l * d_l, axis=1, keepdims=True
            )
            ds_m = (p_m * (d_m - delta)).astype(jnp.bfloat16)
            ds_l = (p_l * (d_l - delta)).astype(jnp.bfloat16)
            gq[rows, cols] = ((dot_nn(ds_m, mk) + dot_nn(ds_l, lk)) * scale).astype(jnp.bfloat16)

    per = n // parts

    def shards(p):
        return pl.ds(p * per, per)

    def rs_s(d, p):
        return remote(
            p_send.at[d, shards(p)], s_recv.at[d, shards(p)],
            r_ssend.at[d, p], r_srecv.at[d, p], me, sib,
        )

    def rs_y(d, p):
        return remote(
            y_send.at[d, shards(p)], y_recv.at[d, shards(p)],
            r_ysend.at[d, p], r_yrecv.at[d, p], me, lax.rem(mf + 2 * d, nf),
        )

    def queries_of(f):
        for i in range(rows_dev // BLK):
            attend(f * (rows_dev // BLK) + i)

    def share(f, dst, d, p):
        grad = gq[pl.ds(pl.multiple_of(f * rows_dev, rows_dev), rows_dev), :]

        @pl.loop(p * per, (p + 1) * per)
        def _(m):
            dst[d, m] = dot_nt(grad, wf[m]).astype(jnp.bfloat16)

    @pl.loop(0, ny)
    def _(i):
        d = lax.rem(i + 1, ny)
        f_sib = lax.rem(sib + 2 * d, nf)
        f_own = lax.rem(mf + 2 * d, nf)
        queries_of(f_sib)
        for p in range(parts):
            share(f_sib, p_send, d, p)
            rs_s(d, p).start()
        queries_of(f_own)
        for p in range(parts):
            share(f_own, p_own, d, p)
            rs_s(d, p).wait_recv()

            @pl.when(d > 0)
            def _():
                for m in range(p * per, (p + 1) * per):
                    y_send[d, m] = (
                        p_own[d, m].astype(jnp.float32) + s_recv[d, m].astype(jnp.float32)
                    ).astype(jnp.bfloat16)
                rs_y(d, p).start()

    for p in range(parts):
        for d in range(1, ny):
            rs_y(d, p).wait_recv()
    for m in range(n):
        total = p_own[0, m].astype(jnp.float32) + s_recv[0, m].astype(jnp.float32)
        for d in range(1, ny):
            total = total + y_recv[d, m].astype(jnp.float32)
        gin_ref[:, m * dk:(m + 1) * dk] = total.astype(jnp.bfloat16)

    @pl.loop(1, n)
    def _(d):
        peer = lax.rem(me + d, n)
        id_copy(peer, me).wait_send()
        block_copy(peer, me).wait_send()

    for zz in range(nz):
        @pl.when((zz <= z) & (z + 1 < nz))
        def _():
            w_up_copy(zz).wait_send()

        @pl.when((zz >= z) & (z > 0))
        def _():
            w_down_copy(zz).wait_send()

        for r in range(nx - 1):
            w_x_copy(r, zz).wait_send()
    for d in range(ny):
        if d:
            x_ycopy(d).wait_send()
        x_scopy(lax.rem(mf + 2 * d, nf)).wait_send()
        for p in range(parts):
            rs_s(d, p).wait_send()
            if d:
                rs_y(d, p).wait_send()


def local(n, nf, layer_input, w_query, local_kv, memory_kv, memory_ids, grad_out):
    nx = 2 ** ((n.bit_length() - 1) // 2)
    nz = n // nx
    ny = nf // 2
    rows_dev, d_model = layer_input.shape
    dk, width = w_query.shape
    ctx = rows_dev * nf
    tiles, topk = memory_ids.shape
    mb_dev = memory_kv.shape[0]
    flat = memory_ids.reshape(1, tiles * topk)
    ids_v = jnp.pad(flat, ((0, 7), (0, 128 - tiles * topk)))
    bf, f32, i32 = jnp.bfloat16, jnp.float32, jnp.int32
    any_spec = pl.BlockSpec(memory_space=pl.ANY)
    vmem_spec = pl.BlockSpec(memory_space=pltpu.VMEM)
    dma = pltpu.SemaphoreType.DMA
    heads = width // HD
    pre = 2 * heads * ctx * (n * BLK + ctx) * 4 <= 25 * 1024 * 1024
    parts = math.gcd(n, 4)
    mem_grid = pltpu.VMEM((heads, n, ctx, BLK) if pre else (8, 128), f32)
    loc_grid = pltpu.VMEM((heads, ctx, ctx) if pre else (8, 128), f32)
    part = pltpu.VMEM((ny, n, rows_dev, dk), bf)
    return pl.pallas_call(
        functools.partial(kernel, n, nx, nf, topk, mb_dev, pre, parts),
        out_shape=(
            jax.ShapeDtypeStruct((ctx, width), bf),
            jax.ShapeDtypeStruct((rows_dev, d_model), bf),
        ),
        in_specs=[pl.BlockSpec(memory_space=pltpu.SMEM), vmem_spec] + [any_spec] * 5,
        out_specs=(vmem_spec, vmem_spec),
        scratch_shapes=[
            pltpu.VMEM((n, dk, width), bf),
            pltpu.VMEM((ctx, d_model), bf),
            pltpu.VMEM(memory_kv.shape, bf),
            pltpu.VMEM(local_kv.shape, bf),
            pltpu.VMEM(grad_out.shape, bf),
            pltpu.VMEM((n,) + memory_kv.shape[1:], bf),
            pltpu.VMEM((n, 8, 128), i32),
            pltpu.VMEM((n,) + memory_kv.shape[1:], bf),
            pltpu.SMEM((n, 8, 128), i32),
            pltpu.VMEM((ctx, width), f32),
            pltpu.VMEM((ctx, width), bf),
            pltpu.VMEM((ctx, width), bf),
            part, part, part, part, part, mem_grid, mem_grid, loc_grid, loc_grid,
            dma((5,)), dma((n,)), dma((n,)), dma((1,)),
            dma((nz,)), dma((nz,)), dma((max(nx - 1, 1), nz)), dma((nz,)),
            dma((max(nx - 1, 1), nz)),
            dma((ny,)), dma((nf,)), dma((nf,)), dma((n,)), dma((n,)),
            dma((ny, parts)), dma((ny, parts)), dma((ny, parts)), dma((ny, parts)),
        ],
        compiler_params=pltpu.CompilerParams(
            collective_id=0, has_side_effects=True, vmem_limit_bytes=62 * 1024 * 1024
        ),
    )(memory_ids, ids_v, layer_input, w_query, local_kv, memory_kv, grad_out)


def solution(mesh):
    placed = (
        P(("mem", "fsdp"), None),
        P("mem", "fsdp"),
        P(None, "mem", "fsdp"),
        P("mem", None, None, "fsdp"),
        P("mem", None),
        P("mem", "fsdp"),
    )
    return jax.shard_map(
        functools.partial(local, mesh.shape["mem"], mesh.shape["fsdp"]),
        mesh=mesh,
        in_specs=placed,
        out_specs=(P("mem", "fsdp"), P(("mem", "fsdp"), None)),
        check_vma=False,
    )
```

```python
import functools
import math

import jax
import jax.numpy as jnp
from jax import lax
from jax.experimental import pallas as pl
from jax.experimental.pallas import tpu as pltpu
from jax.sharding import PartitionSpec as P

HD = 128
BLK = 128
NEG_FILL = -1e30
MESH = pl.DeviceIdType.MESH
NT = (((1,), (1,)), ((), ()))


def dot_nn(a, b):
    return jnp.dot(a, b, preferred_element_type=jnp.float32)


def dot_nt(a, b):
    return lax.dot_general(a, b, NT, preferred_element_type=jnp.float32)


def kernel(
    n, nx, nf, topk, mb_dev, pre, parts,
    ids_s, ids_v, x_hbm, w_hbm, lkv_hbm, mkv_hbm, go_hbm,
    att_ref, gin_ref,
    wf, xf, kv, lkv, go, outbox, inbox, ids_in, ids_sm, q32, qb, gq,
    p_send, p_own, s_recv, y_send, y_recv, s_mem, d_mem, s_loc, d_loc,
    l_sem, i_send, i_recv, i_loc, w_up, w_down, w_x, w_recv, wx_recv,
    x_ysend, x_ssend, x_recv, m_send, m_recv, r_ssend, r_srecv, r_ysend, r_yrecv,
):
    me = lax.axis_index("mem")
    mf = lax.axis_index("fsdp")
    nz = n // nx
    z, xx = me // nx, lax.rem(me, nx)
    ny = nf // 2
    yy, cc = mf // 2, lax.rem(mf, 2)
    sib = mf + 1 - 2 * cc
    dk = wf.shape[1]
    width = wf.shape[2]
    heads = width // HD
    tiles = ids_s.shape[0]
    rows_dev = xf.shape[0] // nf
    ctx = xf.shape[0]

    def local_copy(src, dst, k):
        return pltpu.make_async_copy(src, dst, l_sem.at[k])

    own_x = pl.ds(pl.multiple_of(mf * rows_dev, rows_dev), rows_dev)
    c_w = local_copy(w_hbm, wf.at[me], 0)
    c_x = local_copy(x_hbm, xf.at[own_x, :], 1)
    c_kv = local_copy(mkv_hbm, kv, 2)
    c_lkv = local_copy(lkv_hbm, lkv, 3)
    c_go = local_copy(go_hbm, go, 4)
    c_w.start()
    c_x.start()
    c_kv.start()
    c_lkv.start()
    c_go.start()

    barrier = pltpu.get_barrier_semaphore()

    @pl.loop(1, n)
    def _(d):
        pl.semaphore_signal(
            barrier, inc=1, device_id=(lax.rem(me + d, n), mf), device_id_type=MESH
        )

    pl.semaphore_signal(barrier, inc=1, device_id=(me, sib), device_id_type=MESH)
    for d in range(1, ny):
        pl.semaphore_signal(
            barrier, inc=1, device_id=(me, lax.rem(mf + 2 * d, nf)), device_id_type=MESH
        )
    pl.semaphore_wait(barrier, n - 1 + 1 + ny - 1)

    def remote(src, dst, s, r, dm, df):
        return pltpu.make_async_remote_copy(
            src_ref=src, dst_ref=dst, send_sem=s, recv_sem=r,
            device_id=(dm, df), device_id_type=MESH,
        )

    def id_copy(peer, slot):
        return remote(ids_v, inbox.at[slot], i_send.at[peer], i_recv.at[slot], peer, mf)

    @pl.loop(1, n)
    def _(d):
        id_copy(lax.rem(me + d, n), me).start()

    def w_copy(slot, sem, dst_m, rsem):
        return remote(wf.at[slot], wf.at[slot], sem, rsem, dst_m, mf)

    def w_up_copy(zz):
        return w_copy(zz * nx + xx, w_up.at[zz], me + nx, w_recv.at[zz])

    def w_down_copy(zz):
        return w_copy(zz * nx + xx, w_down.at[zz], me - nx, w_recv.at[zz])

    x_next = z * nx + lax.rem(xx + 1, nx)

    def w_x_copy(r, zz):
        slot = zz * nx + lax.rem(xx - r + nx, nx)
        return w_copy(slot, w_x.at[r, zz], x_next, wx_recv.at[r, zz])

    def w_x_arrival(r, zz):
        slot = zz * nx + lax.rem(xx - 1 - r + 2 * nx, nx)
        return w_copy(slot, w_x.at[r, zz], x_next, wx_recv.at[r, zz])

    c_w.wait()

    @pl.when(z + 1 < nz)
    def _():
        w_up_copy(z).start()

    @pl.when(z > 0)
    def _():
        w_down_copy(z).start()

    w_x_copy(0, z).start()
    c_x.wait()

    def x_rows(f):
        return xf.at[pl.ds(pl.multiple_of(f * rows_dev, rows_dev), rows_dev), :]

    def x_ycopy(d):
        return remote(
            x_rows(mf), x_rows(mf), x_ysend.at[d], x_recv.at[mf], me, lax.rem(mf + 2 * d, nf)
        )

    def x_scopy(f):
        return remote(x_rows(f), x_rows(f), x_ssend.at[f], x_recv.at[f], me, sib)

    for d in range(1, ny):
        x_ycopy(d).start()
    x_scopy(mf).start()

    @pl.loop(1, n)
    def _(d):
        src = lax.rem(me + d, n)
        id_copy(src, src).wait_recv()

    c_ids = pltpu.make_async_copy(inbox, ids_sm, i_loc.at[0])
    c_ids.start()
    c_kv.wait()
    c_ids.wait()

    @pl.loop(1, n)
    def _(d):
        peer = lax.rem(me + d, n)
        want = jnp.int32(0)
        for j in range(tiles * topk):
            one = ids_sm[peer, 0, j]
            want = jnp.where(one // mb_dev == me, lax.rem(one, mb_dev), want)
        outbox[peer] = kv[want]

    mine = jnp.int32(0)
    for j in range(tiles * topk):
        one = ids_s[j // topk, j % topk]
        mine = jnp.where(one // mb_dev == me, lax.rem(one, mb_dev), mine)
    ids_in[me] = kv[mine]

    def block_copy(peer, slot):
        return remote(
            outbox.at[peer], ids_in.at[slot], m_send.at[peer], m_recv.at[slot], peer, mf
        )

    def send_blocks(k):
        @pl.loop(1, n)
        def _(d):
            peer = lax.rem(me + d, n)
            column = lax.rem(peer, nx) == xx

            @pl.when((column & (k == 3)) | (jnp.logical_not(column) & (k == 2)))
            def _():
                block_copy(peer, me).start()

    for k in range(1, nz):
        @pl.when(z - k >= 0)
        def _():
            w_up_copy(z - k).wait_recv()

            @pl.when(z + 1 < nz)
            def _():
                w_up_copy(z - k).start()

            w_x_copy(0, z - k).start()

        @pl.when(z + k < nz)
        def _():
            w_down_copy(z + k).wait_recv()

            @pl.when(z > 0)
            def _():
                w_down_copy(z + k).start()

            w_x_copy(0, z + k).start()

        send_blocks(k)

    for d in range(1, ny):
        f = lax.rem(mf + 2 * d, nf)
        x_scopy(f).wait_recv()
        x_scopy(f).start()
    for d in range(ny):
        x_scopy(lax.rem(sib + 2 * d, nf)).wait_recv()

    q32[...] = jnp.zeros_like(q32)

    def project(slot):
        q32[...] += dot_nn(xf[:, pl.ds(pl.multiple_of(slot * dk, dk), dk)], wf[slot])

    def by_distance(body):
        body(z)
        for k in range(1, nz):
            for zz in (z - k, z + k):
                @pl.when((zz >= 0) & (zz < nz))
                def _():
                    body(zz)

    @pl.loop(0, nz)
    def _(zz):
        project(zz * nx + xx)

    for r in range(nx - 1):
        def arrived(zz):
            w_x_arrival(r, zz).wait_recv()
            if r + 1 < nx - 1:
                w_x_copy(r + 1, zz).start()
            project(zz * nx + lax.rem(xx - 1 - r + 2 * nx, nx))

        by_distance(arrived)

    qb[...] = q32[...].astype(jnp.bfloat16)
    c_lkv.wait()
    c_go.wait()

    scale = 1.0 / math.sqrt(HD)

    def head_cols(h):
        return pl.ds(pl.multiple_of(h * HD, HD), HD)

    def block_scores(o):
        @pl.loop(0, heads)
        def _(h):
            cols = head_cols(h)
            s_mem[h, o] = dot_nt(qb[:, cols], ids_in[o, 0, :, cols]) * scale
            d_mem[h, o] = dot_nt(go[:, cols], ids_in[o, 1, :, cols])

    if pre:
        @pl.loop(0, heads)
        def _(h):
            cols = head_cols(h)
            causal = lax.broadcasted_iota(jnp.int32, (ctx, ctx), 0) >= (
                lax.broadcasted_iota(jnp.int32, (ctx, ctx), 1)
            )
            s_loc[h] = jnp.where(causal, dot_nt(qb[:, cols], lkv[0, :, cols]) * scale, NEG_FILL)
            d_loc[h] = dot_nt(go[:, cols], lkv[1, :, cols])

        block_scores(me)

    @pl.loop(1, n)
    def _(d):
        src = lax.rem(me + d, n)
        block_copy(src, src).wait_recv()
        if pre:
            block_scores(src)

    def attend(t):
        rows = pl.ds(pl.multiple_of(t * BLK, BLK), BLK)
        owners = [ids_s[t, j] // mb_dev for j in range(topk)]

        @pl.loop(0, heads)
        def _(h):
            cols = head_cols(h)
            mk = jnp.concatenate([ids_in[o, 0, :, cols] for o in owners], axis=0)
            mv = jnp.concatenate([ids_in[o, 1, :, cols] for o in owners], axis=0)
            lk = lkv[0, :, cols]
            lv = lkv[1, :, cols]
            if pre:
                s_m = jnp.concatenate([s_mem[h, o, rows, :] for o in owners], axis=1)
                d_m = jnp.concatenate([d_mem[h, o, rows, :] for o in owners], axis=1)
                s_l = s_loc[h, rows, :]
                d_l = d_loc[h, rows, :]
            else:
                q = qb[rows, cols]
                g = go[rows, cols]
                causal = lax.broadcasted_iota(jnp.int32, (BLK, ctx), 0) + t * BLK >= (
                    lax.broadcasted_iota(jnp.int32, (BLK, ctx), 1)
                )
                s_m = dot_nt(q, mk) * scale
                s_l = jnp.where(causal, dot_nt(q, lk) * scale, NEG_FILL)
                d_m = dot_nt(g, mv)
                d_l = dot_nt(g, lv)
            top = jnp.maximum(
                jnp.max(s_m, axis=1, keepdims=True), jnp.max(s_l, axis=1, keepdims=True)
            )
            e_m = jnp.exp(s_m - top)
            e_l = jnp.exp(s_l - top)
            inv = 1.0 / (
                jnp.sum(e_m, axis=1, keepdims=True) + jnp.sum(e_l, axis=1, keepdims=True)
            )
            p_m = e_m * inv
            p_l = e_l * inv
            att_ref[rows, cols] = (
                dot_nn(p_m.astype(jnp.bfloat16), mv) + dot_nn(p_l.astype(jnp.bfloat16), lv)
            ).astype(jnp.bfloat16)
            delta = jnp.sum(p_m * d_m, axis=1, keepdims=True) + jnp.sum(
                p_l * d_l, axis=1, keepdims=True
            )
            ds_m = (p_m * (d_m - delta)).astype(jnp.bfloat16)
            ds_l = (p_l * (d_l - delta)).astype(jnp.bfloat16)
            gq[rows, cols] = ((dot_nn(ds_m, mk) + dot_nn(ds_l, lk)) * scale).astype(jnp.bfloat16)

    per = n // parts

    def shards(p):
        return pl.ds(p * per, per)

    def rs_s(d, p):
        return remote(
            p_send.at[d, shards(p)], s_recv.at[d, shards(p)],
            r_ssend.at[d, p], r_srecv.at[d, p], me, sib,
        )

    def rs_y(d, p):
        return remote(
            y_send.at[d, shards(p)], y_recv.at[d, shards(p)],
            r_ysend.at[d, p], r_yrecv.at[d, p], me, lax.rem(mf + 2 * d, nf),
        )

    def queries_of(f):
        for i in range(rows_dev // BLK):
            attend(f * (rows_dev // BLK) + i)

    def share(f, dst, d, p):
        grad = gq[pl.ds(pl.multiple_of(f * rows_dev, rows_dev), rows_dev), :]

        @pl.loop(p * per, (p + 1) * per)
        def _(m):
            dst[d, m] = dot_nt(grad, wf[m]).astype(jnp.bfloat16)

    @pl.loop(0, ny)
    def _(i):
        d = lax.rem(i + 1, ny)
        f_sib = lax.rem(sib + 2 * d, nf)
        f_own = lax.rem(mf + 2 * d, nf)
        queries_of(f_sib)
        for p in range(parts):
            share(f_sib, p_send, d, p)
            rs_s(d, p).start()
        queries_of(f_own)
        for p in range(parts):
            share(f_own, p_own, d, p)
            rs_s(d, p).wait_recv()

            @pl.when(d > 0)
            def _():
                for m in range(p * per, (p + 1) * per):
                    y_send[d, m] = (
                        p_own[d, m].astype(jnp.float32) + s_recv[d, m].astype(jnp.float32)
                    ).astype(jnp.bfloat16)
                rs_y(d, p).start()

    for p in range(parts):
        for d in range(1, ny):
            rs_y(d, p).wait_recv()
    for m in range(n):
        total = p_own[0, m].astype(jnp.float32) + s_recv[0, m].astype(jnp.float32)
        for d in range(1, ny):
            total = total + y_recv[d, m].astype(jnp.float32)
        gin_ref[:, m * dk:(m + 1) * dk] = total.astype(jnp.bfloat16)

    @pl.loop(1, n)
    def _(d):
        peer = lax.rem(me + d, n)
        id_copy(peer, me).wait_send()
        block_copy(peer, me).wait_send()

    for zz in range(nz):
        @pl.when((zz <= z) & (z + 1 < nz))
        def _():
            w_up_copy(zz).wait_send()

        @pl.when((zz >= z) & (z > 0))
        def _():
            w_down_copy(zz).wait_send()

        for r in range(nx - 1):
            w_x_copy(r, zz).wait_send()
    for d in range(ny):
        if d:
            x_ycopy(d).wait_send()
        x_scopy(lax.rem(mf + 2 * d, nf)).wait_send()
        for p in range(parts):
            rs_s(d, p).wait_send()
            if d:
                rs_y(d, p).wait_send()


def local(n, nf, layer_input, w_query, local_kv, memory_kv, memory_ids, grad_out):
    nx = 2 ** ((n.bit_length() - 1) // 2)
    nz = n // nx
    ny = nf // 2
    rows_dev, d_model = layer_input.shape
    dk, width = w_query.shape
    ctx = rows_dev * nf
    tiles, topk = memory_ids.shape
    mb_dev = memory_kv.shape[0]
    flat = memory_ids.reshape(1, tiles * topk)
    ids_v = jnp.pad(flat, ((0, 7), (0, 128 - tiles * topk)))
    bf, f32, i32 = jnp.bfloat16, jnp.float32, jnp.int32
    any_spec = pl.BlockSpec(memory_space=pl.ANY)
    vmem_spec = pl.BlockSpec(memory_space=pltpu.VMEM)
    dma = pltpu.SemaphoreType.DMA
    heads = width // HD
    pre = 2 * heads * ctx * (n * BLK + ctx) * 4 <= 25 * 1024 * 1024
    parts = math.gcd(n, 4)
    mem_grid = pltpu.VMEM((heads, n, ctx, BLK) if pre else (8, 128), f32)
    loc_grid = pltpu.VMEM((heads, ctx, ctx) if pre else (8, 128), f32)
    part = pltpu.VMEM((ny, n, rows_dev, dk), bf)
    return pl.pallas_call(
        functools.partial(kernel, n, nx, nf, topk, mb_dev, pre, parts),
        out_shape=(
            jax.ShapeDtypeStruct((ctx, width), bf),
            jax.ShapeDtypeStruct((rows_dev, d_model), bf),
        ),
        in_specs=[pl.BlockSpec(memory_space=pltpu.SMEM), vmem_spec] + [any_spec] * 5,
        out_specs=(vmem_spec, vmem_spec),
        scratch_shapes=[
            pltpu.VMEM((n, dk, width), bf),
            pltpu.VMEM((ctx, d_model), bf),
            pltpu.VMEM(memory_kv.shape, bf),
            pltpu.VMEM(local_kv.shape, bf),
            pltpu.VMEM(grad_out.shape, bf),
            pltpu.VMEM((n,) + memory_kv.shape[1:], bf),
            pltpu.VMEM((n, 8, 128), i32),
            pltpu.VMEM((n,) + memory_kv.shape[1:], bf),
            pltpu.SMEM((n, 8, 128), i32),
            pltpu.VMEM((ctx, width), f32),
            pltpu.VMEM((ctx, width), bf),
            pltpu.VMEM((ctx, width), bf),
            part, part, part, part, part, mem_grid, mem_grid, loc_grid, loc_grid,
            dma((5,)), dma((n,)), dma((n,)), dma((1,)),
            dma((nz,)), dma((nz,)), dma((max(nx - 1, 1), nz)), dma((nz,)),
            dma((max(nx - 1, 1), nz)),
            dma((ny,)), dma((nf,)), dma((nf,)), dma((n,)), dma((n,)),
            dma((ny, parts)), dma((ny, parts)), dma((ny, parts)), dma((ny, parts)),
        ],
        compiler_params=pltpu.CompilerParams(
            collective_id=0, has_side_effects=True, vmem_limit_bytes=62 * 1024 * 1024
        ),
    )(memory_ids, ids_v, layer_input, w_query, local_kv, memory_kv, grad_out)


def solution(mesh):
    placed = (
        P(("mem", "fsdp"), None),
        P("mem", "fsdp"),
        P(None, "mem", "fsdp"),
        P("mem", None, None, "fsdp"),
        P("mem", None),
        P("mem", "fsdp"),
    )
    return jax.shard_map(
        functools.partial(local, mesh.shape["mem"], mesh.shape["fsdp"]),
        mesh=mesh,
        in_specs=placed,
        out_specs=(P("mem", "fsdp"), P(("mem", "fsdp"), None)),
        check_vma=False,
    )
```

```python
import functools
import math

import jax
import jax.numpy as jnp
from jax import lax
from jax.experimental import pallas as pl
from jax.experimental.pallas import tpu as pltpu
from jax.sharding import PartitionSpec as P

HD = 128
BLK = 128
NEG_FILL = -1e30
MESH = pl.DeviceIdType.MESH
NT = (((1,), (1,)), ((), ()))


def dot_nn(a, b):
    return jnp.dot(a, b, preferred_element_type=jnp.float32)


def dot_nt(a, b):
    return lax.dot_general(a, b, NT, preferred_element_type=jnp.float32)


def kernel(
    n, nx, nf, topk, mb_dev, pre, parts,
    ids_s, ids_v, x_hbm, w_hbm, lkv_hbm, mkv_hbm, go_hbm,
    att_ref, gin_ref,
    wf, xf, kv, lkv, go, outbox, inbox, ids_in, ids_sm, q32, qb, gq,
    p_send, p_own, s_recv, y_send, y_recv, s_loc, d_loc,
    l_sem, i_send, i_recv, i_loc, w_up, w_down, w_x, w_recv, wx_recv,
    x_ysend, x_ssend, x_recv, m_send, m_recv, r_ssend, r_srecv, r_ysend, r_yrecv,
):
    me = lax.axis_index("mem")
    mf = lax.axis_index("fsdp")
    nz = n // nx
    z, xx = me // nx, lax.rem(me, nx)
    ny = nf // 2
    yy, cc = mf // 2, lax.rem(mf, 2)
    sib = mf + 1 - 2 * cc
    dk = wf.shape[1]
    width = wf.shape[2]
    heads = width // HD
    tiles = ids_s.shape[0]
    rows_dev = xf.shape[0] // nf
    ctx = xf.shape[0]

    def local_copy(src, dst, k):
        return pltpu.make_async_copy(src, dst, l_sem.at[k])

    own_x = pl.ds(pl.multiple_of(mf * rows_dev, rows_dev), rows_dev)
    c_w = local_copy(w_hbm, wf.at[me], 0)
    c_x = local_copy(x_hbm, xf.at[own_x, :], 1)
    c_kv = local_copy(mkv_hbm, kv, 2)
    c_lkv = local_copy(lkv_hbm, lkv, 3)
    c_go = local_copy(go_hbm, go, 4)
    c_w.start()
    c_x.start()
    c_kv.start()
    c_lkv.start()
    c_go.start()

    barrier = pltpu.get_barrier_semaphore()

    @pl.loop(1, n)
    def _(d):
        pl.semaphore_signal(
            barrier, inc=1, device_id=(lax.rem(me + d, n), mf), device_id_type=MESH
        )

    pl.semaphore_signal(barrier, inc=1, device_id=(me, sib), device_id_type=MESH)
    for d in range(1, ny):
        pl.semaphore_signal(
            barrier, inc=1, device_id=(me, lax.rem(mf + 2 * d, nf)), device_id_type=MESH
        )
    pl.semaphore_wait(barrier, n - 1 + 1 + ny - 1)

    def remote(src, dst, s, r, dm, df):
        return pltpu.make_async_remote_copy(
            src_ref=src, dst_ref=dst, send_sem=s, recv_sem=r,
            device_id=(dm, df), device_id_type=MESH,
        )

    def id_copy(peer, slot):
        return remote(ids_v, inbox.at[slot], i_send.at[peer], i_recv.at[slot], peer, mf)

    @pl.loop(1, n)
    def _(d):
        id_copy(lax.rem(me + d, n), me).start()

    def w_copy(slot, sem, dst_m, rsem):
        return remote(wf.at[slot], wf.at[slot], sem, rsem, dst_m, mf)

    def w_up_copy(zz):
        return w_copy(zz * nx + xx, w_up.at[zz], me + nx, w_recv.at[zz])

    def w_down_copy(zz):
        return w_copy(zz * nx + xx, w_down.at[zz], me - nx, w_recv.at[zz])

    x_next = z * nx + lax.rem(xx + 1, nx)

    def w_x_copy(r, zz):
        slot = zz * nx + lax.rem(xx - r + nx, nx)
        return w_copy(slot, w_x.at[r, zz], x_next, wx_recv.at[r, zz])

    def w_x_arrival(r, zz):
        slot = zz * nx + lax.rem(xx - 1 - r + 2 * nx, nx)
        return w_copy(slot, w_x.at[r, zz], x_next, wx_recv.at[r, zz])

    c_w.wait()

    @pl.when(z + 1 < nz)
    def _():
        w_up_copy(z).start()

    @pl.when(z > 0)
    def _():
        w_down_copy(z).start()

    w_x_copy(0, z).start()
    c_x.wait()

    def x_rows(f):
        return xf.at[pl.ds(pl.multiple_of(f * rows_dev, rows_dev), rows_dev), :]

    def x_ycopy(d):
        return remote(
            x_rows(mf), x_rows(mf), x_ysend.at[d], x_recv.at[mf], me, lax.rem(mf + 2 * d, nf)
        )

    def x_scopy(f):
        return remote(x_rows(f), x_rows(f), x_ssend.at[f], x_recv.at[f], me, sib)

    for d in range(1, ny):
        x_ycopy(d).start()
    x_scopy(mf).start()

    @pl.loop(1, n)
    def _(d):
        src = lax.rem(me + d, n)
        id_copy(src, src).wait_recv()

    c_ids = pltpu.make_async_copy(inbox, ids_sm, i_loc.at[0])
    c_ids.start()
    c_kv.wait()
    c_ids.wait()

    @pl.loop(1, n)
    def _(d):
        peer = lax.rem(me + d, n)
        want = jnp.int32(0)
        for j in range(tiles * topk):
            one = ids_sm[peer, 0, j]
            want = jnp.where(one // mb_dev == me, lax.rem(one, mb_dev), want)
        outbox[peer] = kv[want]

    mine = jnp.int32(0)
    for j in range(tiles * topk):
        one = ids_s[j // topk, j % topk]
        mine = jnp.where(one // mb_dev == me, lax.rem(one, mb_dev), mine)
    ids_in[me] = kv[mine]

    def block_copy(peer, slot):
        return remote(
            outbox.at[peer], ids_in.at[slot], m_send.at[peer], m_recv.at[slot], peer, mf
        )

    def send_blocks(k):
        @pl.loop(1, n)
        def _(d):
            peer = lax.rem(me + n - d, n)
            column = lax.rem(peer, nx) == xx

            @pl.when((column & (k == 3)) | (jnp.logical_not(column) & (k == 2)))
            def _():
                block_copy(peer, me).start()

    for k in range(1, nz):
        @pl.when(z - k >= 0)
        def _():
            w_up_copy(z - k).wait_recv()

            @pl.when(z + 1 < nz)
            def _():
                w_up_copy(z - k).start()

            w_x_copy(0, z - k).start()

        @pl.when(z + k < nz)
        def _():
            w_down_copy(z + k).wait_recv()

            @pl.when(z > 0)
            def _():
                w_down_copy(z + k).start()

            w_x_copy(0, z + k).start()

        send_blocks(k)

    for d in range(1, ny):
        f = lax.rem(mf + 2 * d, nf)
        x_scopy(f).wait_recv()
        x_scopy(f).start()
    for d in range(ny):
        x_scopy(lax.rem(sib + 2 * d, nf)).wait_recv()

    q32[...] = jnp.zeros_like(q32)

    def project(slot):
        q32[...] += dot_nn(xf[:, pl.ds(pl.multiple_of(slot * dk, dk), dk)], wf[slot])

    def by_distance(body):
        body(z)
        for k in range(1, nz):
            for zz in (z - k, z + k):
                @pl.when((zz >= 0) & (zz < nz))
                def _():
                    body(zz)

    @pl.loop(0, nz)
    def _(zz):
        project(zz * nx + xx)

    for r in range(nx - 1):
        def arrived(zz):
            w_x_arrival(r, zz).wait_recv()
            if r + 1 < nx - 1:
                w_x_copy(r + 1, zz).start()
            project(zz * nx + lax.rem(xx - 1 - r + 2 * nx, nx))

        by_distance(arrived)

    qb[...] = q32[...].astype(jnp.bfloat16)
    c_lkv.wait()
    c_go.wait()

    scale = 1.0 / math.sqrt(HD)

    def head_cols(h):
        return pl.ds(pl.multiple_of(h * HD, HD), HD)

    if pre:
        @pl.loop(0, heads)
        def _(h):
            cols = head_cols(h)
            causal = lax.broadcasted_iota(jnp.int32, (ctx, ctx), 0) >= (
                lax.broadcasted_iota(jnp.int32, (ctx, ctx), 1)
            )
            s_loc[h] = jnp.where(causal, dot_nt(qb[:, cols], lkv[0, :, cols]) * scale, NEG_FILL)
            d_loc[h] = dot_nt(go[:, cols], lkv[1, :, cols])

    @pl.loop(1, n)
    def _(d):
        src = lax.rem(me + d, n)
        block_copy(src, src).wait_recv()

    def attend(t):
        rows = pl.ds(pl.multiple_of(t * BLK, BLK), BLK)
        owners = [ids_s[t, j] // mb_dev for j in range(topk)]

        @pl.loop(0, heads)
        def _(h):
            cols = head_cols(h)
            mk = jnp.concatenate([ids_in[o, 0, :, cols] for o in owners], axis=0)
            mv = jnp.concatenate([ids_in[o, 1, :, cols] for o in owners], axis=0)
            lk = lkv[0, :, cols]
            lv = lkv[1, :, cols]
            if pre:
                s_m = dot_nt(qb[rows, cols], mk) * scale
                d_m = dot_nt(go[rows, cols], mv)
                s_l = s_loc[h, rows, :]
                d_l = d_loc[h, rows, :]
            else:
                q = qb[rows, cols]
                g = go[rows, cols]
                causal = lax.broadcasted_iota(jnp.int32, (BLK, ctx), 0) + t * BLK >= (
                    lax.broadcasted_iota(jnp.int32, (BLK, ctx), 1)
                )
                s_m = dot_nt(q, mk) * scale
                s_l = jnp.where(causal, dot_nt(q, lk) * scale, NEG_FILL)
                d_m = dot_nt(g, mv)
                d_l = dot_nt(g, lv)
            top = jnp.maximum(
                jnp.max(s_m, axis=1, keepdims=True), jnp.max(s_l, axis=1, keepdims=True)
            )
            e_m = jnp.exp(s_m - top)
            e_l = jnp.exp(s_l - top)
            inv = 1.0 / (
                jnp.sum(e_m, axis=1, keepdims=True) + jnp.sum(e_l, axis=1, keepdims=True)
            )
            p_m = e_m * inv
            p_l = e_l * inv
            att_ref[rows, cols] = (
                dot_nn(p_m.astype(jnp.bfloat16), mv) + dot_nn(p_l.astype(jnp.bfloat16), lv)
            ).astype(jnp.bfloat16)
            delta = jnp.sum(p_m * d_m, axis=1, keepdims=True) + jnp.sum(
                p_l * d_l, axis=1, keepdims=True
            )
            ds_m = (p_m * (d_m - delta)).astype(jnp.bfloat16)
            ds_l = (p_l * (d_l - delta)).astype(jnp.bfloat16)
            gq[rows, cols] = ((dot_nn(ds_m, mk) + dot_nn(ds_l, lk)) * scale).astype(jnp.bfloat16)

    per = n // parts

    def shards(p):
        return pl.ds(p * per, per)

    def rs_s(d, p):
        return remote(
            p_send.at[d, shards(p)], s_recv.at[d, shards(p)],
            r_ssend.at[d, p], r_srecv.at[d, p], me, sib,
        )

    def rs_y(d, p):
        return remote(
            y_send.at[d, shards(p)], y_recv.at[d, shards(p)],
            r_ysend.at[d, p], r_yrecv.at[d, p], me, lax.rem(mf + 2 * d, nf),
        )

    def queries_of(f):
        for i in range(rows_dev // BLK):
            attend(f * (rows_dev // BLK) + i)

    def share(f, dst, d, p):
        grad = gq[pl.ds(pl.multiple_of(f * rows_dev, rows_dev), rows_dev), :]

        @pl.loop(p * per, (p + 1) * per)
        def _(m):
            dst[d, m] = dot_nt(grad, wf[m]).astype(jnp.bfloat16)

    @pl.loop(0, ny)
    def _(i):
        d = lax.rem(i + 1, ny)
        f_sib = lax.rem(sib + 2 * d, nf)
        f_own = lax.rem(mf + 2 * d, nf)
        queries_of(f_sib)
        for p in range(parts):
            share(f_sib, p_send, d, p)
            rs_s(d, p).start()
        queries_of(f_own)
        for p in range(parts):
            share(f_own, p_own, d, p)
            rs_s(d, p).wait_recv()

            @pl.when(d > 0)
            def _():
                for m in range(p * per, (p + 1) * per):
                    y_send[d, m] = (
                        p_own[d, m].astype(jnp.float32) + s_recv[d, m].astype(jnp.float32)
                    ).astype(jnp.bfloat16)
                rs_y(d, p).start()

    for p in range(parts):
        for d in range(1, ny):
            rs_y(d, p).wait_recv()
    for m in range(n):
        total = p_own[0, m].astype(jnp.float32) + s_recv[0, m].astype(jnp.float32)
        for d in range(1, ny):
            total = total + y_recv[d, m].astype(jnp.float32)
        gin_ref[:, m * dk:(m + 1) * dk] = total.astype(jnp.bfloat16)

    @pl.loop(1, n)
    def _(d):
        peer = lax.rem(me + d, n)
        id_copy(peer, me).wait_send()
        block_copy(peer, me).wait_send()

    for zz in range(nz):
        @pl.when((zz <= z) & (z + 1 < nz))
        def _():
            w_up_copy(zz).wait_send()

        @pl.when((zz >= z) & (z > 0))
        def _():
            w_down_copy(zz).wait_send()

        for r in range(nx - 1):
            w_x_copy(r, zz).wait_send()
    for d in range(ny):
        if d:
            x_ycopy(d).wait_send()
        x_scopy(lax.rem(mf + 2 * d, nf)).wait_send()
        for p in range(parts):
            rs_s(d, p).wait_send()
            if d:
                rs_y(d, p).wait_send()


def local(n, nf, layer_input, w_query, local_kv, memory_kv, memory_ids, grad_out):
    nx = 2 ** ((n.bit_length() - 1) // 2)
    nz = n // nx
    ny = nf // 2
    rows_dev, d_model = layer_input.shape
    dk, width = w_query.shape
    ctx = rows_dev * nf
    tiles, topk = memory_ids.shape
    mb_dev = memory_kv.shape[0]
    flat = memory_ids.reshape(1, tiles * topk)
    ids_v = jnp.pad(flat, ((0, 7), (0, 128 - tiles * topk)))
    bf, f32, i32 = jnp.bfloat16, jnp.float32, jnp.int32
    any_spec = pl.BlockSpec(memory_space=pl.ANY)
    vmem_spec = pl.BlockSpec(memory_space=pltpu.VMEM)
    dma = pltpu.SemaphoreType.DMA
    heads = width // HD
    pre = 2 * heads * ctx * ctx * 4 <= 12 * 1024 * 1024
    parts = math.gcd(n, 4)
    loc_grid = pltpu.VMEM((heads, ctx, ctx) if pre else (8, 128), f32)
    part = pltpu.VMEM((ny, n, rows_dev, dk), bf)
    return pl.pallas_call(
        functools.partial(kernel, n, nx, nf, topk, mb_dev, pre, parts),
        out_shape=(
            jax.ShapeDtypeStruct((ctx, width), bf),
            jax.ShapeDtypeStruct((rows_dev, d_model), bf),
        ),
        in_specs=[pl.BlockSpec(memory_space=pltpu.SMEM), vmem_spec] + [any_spec] * 5,
        out_specs=(vmem_spec, vmem_spec),
        scratch_shapes=[
            pltpu.VMEM((n, dk, width), bf),
            pltpu.VMEM((ctx, d_model), bf),
            pltpu.VMEM(memory_kv.shape, bf),
            pltpu.VMEM(local_kv.shape, bf),
            pltpu.VMEM(grad_out.shape, bf),
            pltpu.VMEM((n,) + memory_kv.shape[1:], bf),
            pltpu.VMEM((n, 8, 128), i32),
            pltpu.VMEM((n,) + memory_kv.shape[1:], bf),
            pltpu.SMEM((n, 8, 128), i32),
            pltpu.VMEM((ctx, width), f32),
            pltpu.VMEM((ctx, width), bf),
            pltpu.VMEM((ctx, width), bf),
            part, part, part, part, part, loc_grid, loc_grid,
            dma((5,)), dma((n,)), dma((n,)), dma((1,)),
            dma((nz,)), dma((nz,)), dma((max(nx - 1, 1), nz)), dma((nz,)),
            dma((max(nx - 1, 1), nz)),
            dma((ny,)), dma((nf,)), dma((nf,)), dma((n,)), dma((n,)),
            dma((ny, parts)), dma((ny, parts)), dma((ny, parts)), dma((ny, parts)),
        ],
        compiler_params=pltpu.CompilerParams(
            collective_id=0, has_side_effects=True, vmem_limit_bytes=62 * 1024 * 1024
        ),
    )(memory_ids, ids_v, layer_input, w_query, local_kv, memory_kv, grad_out)


def solution(mesh):
    placed = (
        P(("mem", "fsdp"), None),
        P("mem", "fsdp"),
        P(None, "mem", "fsdp"),
        P("mem", None, None, "fsdp"),
        P("mem", None),
        P("mem", "fsdp"),
    )
    return jax.shard_map(
        functools.partial(local, mesh.shape["mem"], mesh.shape["fsdp"]),
        mesh=mesh,
        in_specs=placed,
        out_specs=(P("mem", "fsdp"), P(("mem", "fsdp"), None)),
        check_vma=False,
    )
```
